32 devices in a mesh: dp: 2 (over y), tensor: 8 (over z, core), fisher: 2 (over x).
Axes of the slice: x: 2, y: 2, z: 4, core: 2. Of those that a mesh axis runs over, the one named last changes fastest.
Arguments:
- train_inputs: bfloat16 [44, 257, 1280], P('dp', None, 'fisher'), may hold values from -6 to 6
- train_cotangents: bfloat16 [44, 257, 3840], P('dp', None, 'tensor'), may hold values from -6 to 6
- train_ids: int32 [44], P('dp'), may hold values from 0 to 15
- query_projection_inputs: bfloat16 [8, 257, 1280], P('tensor', None, 'fisher'), may hold values from -6 to 6
- query_output_cotangents: bfloat16 [8, 257, 3840], P('tensor'), may hold values from -6 to 6
- query_ids: int32 [8], replicated, may hold values from 0 to 15
- fisher_diagonal_weight: bfloat16 [2, 3840, 1280], P(None, 'tensor', 'fisher'), may hold values from 0.049804688 to 2
- layer_index: int32 [16], replicated, may hold values from 0 to 1
Outputs:
- influence: float32 [16, 16, 16], P(('dp', 'fisher'), None, 'tensor')
The draws below stay inside these ranges and needn't reach their ends.
All inputs are finite; a program needn't handle non-finite values.
Results may differ from the reference program's by a relative error of at most 0.004.
Values may be sent and summed in bfloat16 or wider, within the bound.
A program may use at most 128 MiB of HBM per device.

```python
import math
import jax
import jax.numpy as jnp
from jax import lax

D = 1280
HEADS = 16
HEAD_DIM = 80
SEQ = 257
QIDS = 16
LAYERS = 2
TRAIN = 44
QUERIES = 8
TIDS = 16


def plant(drawn, rng, least, top_value):
    longest = drawn.shape.index(max(drawn.shape))
    spots = []
    for shift in (0, 1):
        where = [jax.random.randint(jax.random.fold_in(rng, axis), (), 0, length) for axis, length in enumerate(drawn.shape)]
        where[longest] = (where[longest] + shift) % drawn.shape[longest]
        spots.append(tuple(where))
    return drawn.at[spots[0]].set(least).at[spots[1]].set(top_value)


def block_scale(own_key, extent, pieces, low, high):
    factor_of, own = 1.0, jax.random.fold_in(own_key, 6)
    for axis_at, blocks in pieces:
        heights = jnp.exp(jax.random.uniform(jax.random.fold_in(own, axis_at), (blocks,), jnp.float32, low / len(pieces), high / len(pieces)))
        factor_of = factor_of * jnp.repeat(heights, extent[axis_at] // blocks).reshape([-1 if axis == axis_at else 1 for axis in range(len(extent))])
    return factor_of


def centred(key, extent, width, limit, split=(), held_as=jnp.bfloat16):
    drawn = jax.random.normal(key, extent, jnp.float32) * width
    if len(split) > 0:
        drawn = block_scale(key, extent, split, -0.22, 0.18) * drawn
    return jnp.clip(drawn, min=-limit, max=limit).astype(held_as)


def setup_inputs(seed: int = 0) -> dict:
    key_of = jax.random.split(jax.random.key(seed), 9)
    train_inputs = centred(key_of[0], (TRAIN, SEQ, D), 1.0, 6.0, ((0, 2), (2, 2)))
    train_cotangents = centred(key_of[1], (TRAIN, SEQ, 3 * HEADS * HEAD_DIM), 1.0, 6.0, ((0, 2), (2, 8)))
    train_ids = plant(jax.random.randint(key_of[2], (TRAIN,), 0, TIDS), jax.random.fold_in(key_of[2], 1), 0, TIDS - 1).astype(jnp.int32)
    query_projection_inputs = centred(key_of[3], (QUERIES, SEQ, D), 1.0, 6.0, ((0, 8), (2, 2)))
    query_output_cotangents = centred(key_of[4], (QUERIES, SEQ, 3 * HEADS * HEAD_DIM), 1.0, 6.0, ((0, 8),))
    query_ids = plant(jax.random.randint(key_of[5], (QUERIES,), 0, QIDS), jax.random.fold_in(key_of[5], 1), 0, QIDS - 1).astype(jnp.int32)
    fisher_diagonal_weight = jnp.clip(jnp.exp(math.log(2.0) - 3.6927934 * jax.random.uniform(key_of[6], (LAYERS, 3 * HEADS * HEAD_DIM, D), jnp.float32) ** block_scale(key_of[6], (LAYERS, 3 * HEADS * HEAD_DIM, D), ((1, 8), (2, 2)), -0.2, 0.2)), 0.049804688, 2.0).astype(jnp.bfloat16)
    layer_index = plant(jax.random.randint(key_of[7], (HEADS,), 0, LAYERS), jax.random.fold_in(key_of[7], 1), 0, LAYERS - 1).astype(jnp.int32)
    return dict(train_inputs=train_inputs, train_cotangents=train_cotangents, train_ids=train_ids, query_projection_inputs=query_projection_inputs, query_output_cotangents=query_output_cotangents, query_ids=query_ids, fisher_diagonal_weight=fisher_diagonal_weight, layer_index=layer_index)


def reference(train_inputs, train_cotangents, train_ids, query_projection_inputs, query_output_cotangents, query_ids, fisher_diagonal_weight, layer_index):
    head_width = 3 * HEAD_DIM
    scale_factor = 1.0 / (SEQ * math.sqrt(3 * HEAD_DIM * D))
    stacked = fisher_diagonal_weight.astype(jnp.float32).reshape(LAYERS, HEADS, head_width, D)
    picked = (layer_index[None, :] == jnp.arange(LAYERS, dtype=jnp.int32)[:, None]).astype(jnp.float32)
    fisher_heads = lax.optimization_barrier(jnp.sum(stacked * picked[:, :, None, None], axis=0))
    train_act = train_inputs.astype(jnp.float32)
    query_activation = query_projection_inputs.astype(jnp.float32)
    train_cot = jnp.moveaxis(train_cotangents.astype(jnp.float32).reshape(TRAIN, SEQ, HEADS, head_width), 2, 0)
    query_cot = jnp.moveaxis(query_output_cotangents.astype(jnp.float32).reshape(QUERIES, SEQ, HEADS, head_width), 2, 0)

    def per_head(operands):
        train_part, query_portion, fisher_part = operands
        train_grad = jnp.einsum('nsr,nsd->nrd', train_part, train_act).astype(jnp.bfloat16)
        query_gradient = jnp.einsum('kzo,kzj->koj', query_portion, query_activation)
        weighted = (fisher_part[None] * query_gradient).astype(jnp.bfloat16)
        return jnp.einsum('nx,mx->nm', train_grad.reshape(TRAIN, -1).astype(jnp.float32), weighted.reshape(QUERIES, -1).astype(jnp.float32))
    scores = lax.map(per_head, (train_cot, query_cot, fisher_heads)) * scale_factor
    train_hot = (train_ids[:, None] == jnp.arange(TIDS, dtype=jnp.int32)[None, :]).astype(jnp.float32)
    query_hot = (query_ids[:, None] == jnp.arange(QIDS, dtype=jnp.int32)[None, :]).astype(jnp.float32)
    return jnp.einsum('hnm,na,mb->abh', scores, train_hot, query_hot, precision=lax.Precision.HIGHEST)
```

```python
import functools
import math

import jax
import jax.numpy as jnp
from jax import lax
from jax.experimental import pallas as pl
from jax.experimental.pallas import tpu as pltpu
from jax.sharding import PartitionSpec as P

HEAD_DIM = 80
HEAD_WIDTH = 3 * HEAD_DIM
QIDS = 16
LANES = 128
RB = 16
MESH = pl.DeviceIdType.MESH
F32 = jnp.float32
BF16 = jnp.bfloat16
TN = (((0,), (0,)), ((), ()))
NT = (((1,), (1,)), ((), ()))


def kernel(
    sizes,
    layer_ref,
    tx_hbm,
    tc_hbm,
    qx_hbm,
    qc_hbm,
    fw_hbm,
    tid_ref,
    qid_ref,
    out_ref,
    tx,
    tc,
    grad,
    qc,
    qx,
    weighted,
    fw,
    block,
    acc,
    part,
    got,
    tx_sem,
    tc_sem,
    fw_sem,
    own_sem,
    qc_recv,
    qc_send,
    qx_recv,
    qx_send,
    part_send,
    part_recv,
):
    tensor_n, dp_n, fisher_n, win, ids_dev, scale = sizes
    count, seq, half = tx.shape
    width = tc.shape[2]
    heads = width // HEAD_WIDTH
    total_cols = qc_hbm.shape[2]
    stored = fw.shape[0]
    groups = dp_n * fisher_n
    chips = tensor_n // 2

    dp = lax.axis_index("dp")
    t = lax.axis_index("tensor")
    f = lax.axis_index("fisher")
    a = lax.rem(dp, 2)
    dp_other = dp + 1 - 2 * a
    f_other = 1 - f
    core = lax.rem(t, 2)
    t_other = t + 1 - 2 * core
    me = dp * fisher_n + f

    def start_of(dest):
        first = lax.min((dest * width) // LANES * LANES, total_cols - win)
        return pl.multiple_of(first, LANES)

    def window(dest):
        return qc_hbm.at[0, :, pl.ds(start_of(dest), win)]

    def remote(src, dst, send, recv, to):
        return pltpu.make_async_remote_copy(
            src_ref=src, dst_ref=dst, send_sem=send, recv_sem=recv, device_id=to, device_id_type=MESH
        )

    barrier = pltpu.get_barrier_semaphore()
    for k in range(1, tensor_n):
        pl.semaphore_signal(
            barrier, inc=1, device_id={"tensor": lax.rem(t + k, tensor_n)}, device_id_type=MESH
        )
    for d in range(1, groups):
        g = lax.rem(me + d, groups)
        pl.semaphore_signal(
            barrier,
            inc=1,
            device_id={"dp": g // fisher_n, "fisher": lax.rem(g, fisher_n)},
            device_id_type=MESH,
        )

    own_c = pltpu.make_async_copy(window(t), qc.at[t], own_sem.at[0])
    own_x = pltpu.make_async_copy(qx_hbm.at[0], qx.at[t], own_sem.at[1])
    load_f = pltpu.make_async_copy(fw_hbm, fw, fw_sem)

    def load_x(n):
        return pltpu.make_async_copy(tx_hbm.at[n], tx.at[n], tx_sem.at[n])

    def load_c(n):
        return pltpu.make_async_copy(tc_hbm.at[n], tc.at[n], tc_sem.at[n])

    own_c.start()
    own_x.start()

    @pl.loop(0, count)
    def _(n):
        load_x(n).start()
        load_c(n).start()

    load_f.start()
    pl.semaphore_wait(barrier, tensor_n - 1 + groups - 1)

    def on_line(k):
        return jnp.logical_and(a == k % 2, f == (k // 2) % 2)

    def qc_first(k):
        dest = lax.rem(t + tensor_n - k, tensor_n)
        return remote(window(dest), qc.at[t], qc_send.at[0, k], qc_recv.at[t], {"tensor": dest})

    def slot(k):
        return lax.rem(t + k, tensor_n)

    def qc_to_dp(k):
        m = slot(k)
        return remote(qc.at[m], qc.at[m], qc_send.at[1, k], qc_recv.at[m], {"dp": dp_other})

    def qc_to_fisher(k):
        m = slot(k)
        return remote(qc.at[m], qc.at[m], qc_send.at[2, k], qc_recv.at[m], {"fisher": f_other})

    def x_line(j, side):
        source_core = lax.rem(core + side, 2)
        return lax.rem(source_core + j, 2)

    def x_slot(j, side):
        return 2 * lax.rem(t // 2 + j, chips) + lax.rem(core + side, 2)

    def qx_first(j):
        dest = lax.rem(t + tensor_n - 2 * j, tensor_n)
        return remote(qx_hbm.at[0], qx.at[t], qx_send.at[0, j], qx_recv.at[t], {"tensor": dest})

    def qx_partner():
        return remote(qx_hbm.at[0], qx.at[t], qx_send.at[0, 0], qx_recv.at[t], {"tensor": t_other})

    def qx_to_partner(j):
        m = x_slot(j, 0)
        return remote(qx.at[m], qx.at[m], qx_send.at[1, j], qx_recv.at[m], {"tensor": t_other})

    def qx_to_dp(j):
        m = x_slot(j, 0)
        return remote(qx.at[m], qx.at[m], qx_send.at[2, j], qx_recv.at[m], {"dp": dp_other})

    x_order = list(range(1, chips))
    c_order = list(range(1, tensor_n))
    for i in range(max(len(x_order), len(c_order))):
        if i < len(c_order):
            k = c_order[i]

            @pl.when(on_line(k))
            def _(k=k):
                qc_first(k).start()

        if i < len(x_order):
            j = x_order[i]

            @pl.when(a == x_line(j, 0))
            def _(j=j):
                qx_first(j).start()

    qx_partner().start()

    def train(lo, hi):
        @pl.loop(lo, hi)
        def _(n):
            load_x(n).wait()
            load_c(n).wait()
            grad[n] = lax.dot_general(tc[n], tx[n], TN, preferred_element_type=F32).astype(BF16)

    def forward_c(k):
        @pl.when(on_line(k))
        def _():
            qc_to_dp(k).wait_recv()
            qc_to_dp(k).start()
            qc_to_fisher(k).start()

    def forward_x(j):
        @pl.when(a == x_line(j, 0))
        def _():
            qx_to_dp(j).wait_recv()
            qx_to_dp(j).start()
            qx_to_partner(j).start()

    half_c = (len(c_order) + 1) // 2
    cut = count // 3
    train(0, cut)
    for k in c_order[:half_c]:
        forward_c(k)
    for j in x_order[: (len(x_order) + 1) // 2]:
        forward_x(j)
    train(cut, 2 * cut)
    for k in c_order[half_c:]:
        forward_c(k)
    for j in x_order[(len(x_order) + 1) // 2 :]:
        forward_x(j)
    train(2 * cut, count)

    for k in c_order:

        @pl.when(jnp.logical_and(a != k % 2, f == (k // 2) % 2))
        def _(k=k):
            qc_to_fisher(k).wait_recv()
            qc_to_fisher(k).start()

    for j in x_order:

        @pl.when(a != x_line(j, 0))
        def _(j=j):
            qx_to_partner(j).wait_recv()
            qx_to_partner(j).start()

    for k in c_order:

        @pl.when(f != (k // 2) % 2)
        def _(k=k):
            qc_to_fisher(k).wait_recv()

    for j in range(chips):
        m = x_slot(j, 1)
        remote(qx.at[m], qx.at[m], qx_send.at[1, j], qx_recv.at[m], {"tensor": t_other}).wait_recv()

    own_c.wait()
    own_x.wait()
    load_f.wait()

    for h in range(heads):
        rows = pl.ds(h * HEAD_WIDTH, HEAD_WIDTH)
        which = layer_ref[t * heads + h]
        chosen = jnp.zeros((HEAD_WIDTH, half), F32)
        for layer in range(stored):
            chosen += fw[layer, rows, :].astype(F32) * (which == layer).astype(F32)
        fw[0, rows, :] = chosen.astype(BF16)

    shift = pl.multiple_of(t * width - start_of(t), 16)

    @pl.loop(0, tensor_n)
    def _(m):
        block[...] = lax.dot_general(qc[m], qx[m], TN, preferred_element_type=F32)
        weighted[m] = (fw[0].astype(F32) * block[pl.ds(shift, width), :]).astype(BF16)

    rows_n, rows_m = count * RB, tensor_n * RB
    row_id = lax.broadcasted_iota(jnp.int32, (rows_n, rows_m), 0)
    col_id = lax.broadcasted_iota(jnp.int32, (rows_n, rows_m), 1)
    same = (lax.rem(row_id, RB) == lax.rem(col_id, RB)).astype(F32)
    train_hot = (
        lax.broadcasted_iota(jnp.int32, (groups * ids_dev, count), 0) == tid_ref[...]
    ).astype(F32)
    query_hot = (
        lax.broadcasted_iota(jnp.int32, (rows_m, LANES), 1) == qid_ref[...]
    ).astype(F32)
    part[...] = jnp.zeros_like(part)
    for h in range(heads):
        acc[...] = jnp.zeros_like(acc)

        @pl.loop(0, HEAD_WIDTH // RB)
        def _(i):
            rows = pl.ds(pl.multiple_of(h * HEAD_WIDTH + i * RB, RB), RB)
            left = grad[:, rows, :].reshape(rows_n, half)
            right = weighted[:, rows, :].reshape(rows_m, half)
            acc[...] += lax.dot_general(left, right, NT, preferred_element_type=F32)

        kept = (acc[...] * same).reshape(count, RB, rows_m).sum(axis=1)
        by_query = jnp.dot(
            kept, query_hot, preferred_element_type=F32, precision=lax.Precision.HIGHEST
        )
        buckets = (
            jnp.dot(
                train_hot, by_query, preferred_element_type=F32, precision=lax.Precision.HIGHEST
            )
            * scale
        )
        for g in range(groups):
            part[g, h, 0:ids_dev, :] = buckets[g * ids_dev : (g + 1) * ids_dev, :]

    def exchange(d):
        g = lax.rem(me + d, groups)
        to = {"dp": g // fisher_n, "fisher": lax.rem(g, fisher_n)}
        return remote(part.at[g], got.at[d], part_send.at[d], part_recv.at[d], to)

    for d in range(1, groups):
        exchange(d).start()
    total = part[me]
    for d in range(1, groups):
        exchange(d).wait_recv()
        total += got[d]
    out_ref[...] = total

    for d in range(1, groups):
        exchange(d).wait_send()
    for k in c_order:

        @pl.when(on_line(k))
        def _(k=k):
            qc_first(k).wait_send()
            qc_to_dp(k).wait_send()
            qc_to_fisher(k).wait_send()

        @pl.when(jnp.logical_and(a != k % 2, f == (k // 2) % 2))
        def _(k=k):
            qc_to_fisher(k).wait_send()

    qx_partner().wait_send()
    for j in x_order:

        @pl.when(a == x_line(j, 0))
        def _(j=j):
            qx_first(j).wait_send()
            qx_to_dp(j).wait_send()
            qx_to_partner(j).wait_send()

        @pl.when(a != x_line(j, 0))
        def _(j=j):
            qx_to_partner(j).wait_send()


def local(axes, tx, tc, tids, qx, qc, qids, fw, layers):
    tensor_n, dp_n, fisher_n, ids_dev = axes
    count, seq, half = tx.shape
    width = tc.shape[2]
    heads = width // HEAD_WIDTH
    full = half * fisher_n
    scale = 1.0 / (seq * math.sqrt(HEAD_WIDTH * full))
    total_cols = qc.shape[2]
    win = 0
    for dest in range(tensor_n):
        lo = dest * width // LANES * LANES
        win = max(win, -(-(dest * width + width - lo) // LANES) * LANES)
    groups = dp_n * fisher_n
    sizes = (tensor_n, dp_n, fisher_n, win, ids_dev, scale)
    vmem = pl.BlockSpec(memory_space=pltpu.VMEM)
    hbm = pl.BlockSpec(memory_space=pl.ANY)
    dma = pltpu.SemaphoreType.DMA
    out = pl.pallas_call(
        functools.partial(kernel, sizes),
        out_shape=jax.ShapeDtypeStruct((heads, 8, LANES), F32),
        in_specs=[pl.BlockSpec(memory_space=pltpu.SMEM), hbm, hbm, hbm, hbm, hbm, vmem, vmem],
        out_specs=vmem,
        scratch_shapes=[
            pltpu.VMEM((count, seq, half), BF16),
            pltpu.VMEM((count, seq, width), BF16),
            pltpu.VMEM((count, width, half), BF16),
            pltpu.VMEM((tensor_n, seq, win), BF16),
            pltpu.VMEM((tensor_n, seq, half), BF16),
            pltpu.VMEM((tensor_n, width, half), BF16),
            pltpu.VMEM(fw.shape, BF16),
            pltpu.VMEM((win, half), F32),
            pltpu.VMEM((count * RB, tensor_n * RB), F32),
            pltpu.VMEM((groups, heads, 8, LANES), F32),
            pltpu.VMEM((groups, heads, 8, LANES), F32),
            dma((count,)),
            dma((count,)),
            dma,
            dma((2,)),
            dma((tensor_n,)),
            dma((3, tensor_n)),
            dma((tensor_n,)),
            dma((3, tensor_n // 2)),
            dma((groups,)),
            dma((groups,)),
        ],
        compiler_params=pltpu.CompilerParams(
            collective_id=0, has_side_effects=True, vmem_limit_bytes=60 * 1024 * 1024
        ),
    )(layers, tx, tc, qx, qc, fw, tids[None, :], jnp.repeat(qids, RB)[:, None])
    return jnp.transpose(out[:, :ids_dev, :QIDS], (1, 2, 0))


def solution(mesh):
    in_specs = (
        P("dp", None, "fisher"),
        P("dp", None, "tensor"),
        P("dp"),
        P("tensor", None, "fisher"),
        P("tensor", None, None),
        P(),
        P(None, "tensor", "fisher"),
        P(),
    )
    out_specs = P(("dp", "fisher"), None, "tensor")
    axes = (mesh.shape["tensor"], mesh.shape["dp"], mesh.shape["fisher"], 4)
    return jax.shard_map(
        functools.partial(local, axes),
        mesh=mesh,
        in_specs=in_specs,
        out_specs=out_specs,
        check_vma=False,
    )
```

```python
import functools
import math

import jax
import jax.numpy as jnp
from jax import lax
from jax.experimental import pallas as pl
from jax.experimental.pallas import tpu as pltpu
from jax.sharding import PartitionSpec as P

HEAD_DIM = 80
HEAD_WIDTH = 3 * HEAD_DIM
QIDS = 16
LANES = 128
RB = 16
CHUNKS = 4
MESH = pl.DeviceIdType.MESH
F32 = jnp.float32
BF16 = jnp.bfloat16
TN = (((0,), (0,)), ((), ()))
NT = (((1,), (1,)), ((), ()))


def kernel(
    sizes,
    layer_ref,
    tx_hbm,
    tc_hbm,
    qx_hbm,
    qc_hbm,
    fw_hbm,
    tid_ref,
    qid_ref,
    out_ref,
    tx,
    tc,
    grad,
    qc,
    qx,
    weighted,
    fw,
    block,
    acc,
    part,
    got,
    tx_sem,
    tc_sem,
    fw_sem,
    own_sem,
    own_send,
    qc_recv,
    qc_send,
    qx_recv,
    qx_send,
    part_send,
    part_recv,
):
    tensor_n, dp_n, fisher_n, win, ids_dev, scale = sizes
    count, seq, half = tx.shape
    width = tc.shape[2]
    heads = width // HEAD_WIDTH
    total_cols = qc_hbm.shape[2]
    stored = fw.shape[0]
    groups = dp_n * fisher_n
    chips = tensor_n // 2

    dp = lax.axis_index("dp")
    t = lax.axis_index("tensor")
    f = lax.axis_index("fisher")
    a = lax.rem(dp, 2)
    dp_other = dp + 1 - 2 * a
    f_other = 1 - f
    core = lax.rem(t, 2)
    t_other = t + 1 - 2 * core
    me = dp * fisher_n + f

    def start_of(dest):
        first = lax.min((dest * width) // LANES * LANES, total_cols - win)
        return pl.multiple_of(first, LANES)

    step = seq // (16 * CHUNKS) * 16

    def rows_of(p):
        return pl.ds(p * step, step if p + 1 < CHUNKS else seq - p * step)

    def window(dest, p=None):
        rows = slice(None) if p is None else rows_of(p)
        return qc_hbm.at[0, rows, pl.ds(start_of(dest), win)]

    def remote(src, dst, send, recv, to):
        return pltpu.make_async_remote_copy(
            src_ref=src, dst_ref=dst, send_sem=send, recv_sem=recv, device_id=to, device_id_type=MESH
        )

    barrier = pltpu.get_barrier_semaphore()
    for k in range(1, tensor_n):
        pl.semaphore_signal(
            barrier, inc=1, device_id={"tensor": lax.rem(t + k, tensor_n)}, device_id_type=MESH
        )
    for d in range(1, groups):
        g = lax.rem(me + d, groups)
        pl.semaphore_signal(
            barrier,
            inc=1,
            device_id={"dp": g // fisher_n, "fisher": lax.rem(g, fisher_n)},
            device_id_type=MESH,
        )

    own_c = pltpu.make_async_copy(window(t), qc.at[t], own_sem.at[0])
    own_x = pltpu.make_async_copy(qx_hbm.at[0], qx.at[t], own_sem.at[1])
    load_f = pltpu.make_async_copy(fw_hbm, fw, fw_sem)

    def load_x(n):
        return pltpu.make_async_copy(tx_hbm.at[n], tx.at[n], tx_sem.at[n])

    def load_c(n):
        return pltpu.make_async_copy(tc_hbm.at[n], tc.at[n], tc_sem.at[n])

    pl.semaphore_wait(barrier, tensor_n - 1 + groups - 1)

    def base_c(flip_a, flip_f):
        return lax.rem(a + flip_a, 2) + 2 * lax.rem(f + flip_f, 2)

    def slot(k):
        return lax.rem(t + k, tensor_n)

    def target(k):
        return lax.rem(t + tensor_n - k, tensor_n)

    def far(m):
        return m // 2 != t // 2

    def hop(buf, m, p, send, recv, to):
        piece = buf.at[m, rows_of(p), :]
        return remote(piece, piece, send, recv.at[m, p], to)

    def qc_first(k, i, p):
        return remote(
            window(target(k), p),
            qc.at[t, rows_of(p), :],
            qc_send.at[0, i, p],
            qc_recv.at[t, p],
            {"tensor": target(k)},
        )

    def qc_partner():
        return remote(
            window(t_other), qc.at[t], own_send.at[0], qc_recv.at[t, 0], {"tensor": t_other}
        )

    def qc_to_dp(k, i, p):
        return hop(qc, slot(k), p, qc_send.at[1, i, p], qc_recv, {"dp": dp_other})

    def qc_to_fisher(k, i, p, via):
        return hop(qc, slot(k), p, qc_send.at[via, i, p], qc_recv, {"fisher": f_other})

    def base_x(flip):
        return lax.rem(a + core + flip, 2)

    def x_slot(j, side):
        return 2 * lax.rem(t // 2 + j, chips) + lax.rem(core + side, 2)

    def qx_first(j, i, p):
        return remote(
            qx_hbm.at[0, rows_of(p), :],
            qx.at[t, rows_of(p), :],
            qx_send.at[0, i, p],
            qx_recv.at[t, p],
            {"tensor": lax.rem(t + tensor_n - 2 * j, tensor_n)},
        )

    def qx_partner():
        return remote(
            qx_hbm.at[0], qx.at[t], own_send.at[1], qx_recv.at[t, 0], {"tensor": t_other}
        )

    def qx_to_partner(j, i, p, via):
        return hop(qx, x_slot(j, 0), p, qx_send.at[via, i, p], qx_recv, {"tensor": t_other})

    def qx_to_dp(j, i, p):
        return hop(qx, x_slot(j, 0), p, qx_send.at[2, i, p], qx_recv, {"dp": dp_other})

    c_steps, x_steps = tensor_n // 4, chips // 2
    for p in range(CHUNKS):
        for i in range(c_steps):
            k = base_c(0, 0) + 4 * i

            @pl.when(far(target(k)))
            def _(k=k, i=i, p=p):
                qc_first(k, i, p).start()

    for i in range(x_steps):
        j = base_x(0) + 2 * i

        @pl.when(j > 0)
        def _(j=j, i=i):
            for p in range(CHUNKS):
                qx_first(j, i, p).start()

    qc_partner().start()
    qx_partner().start()
    own_c.start()
    own_x.start()
    load_f.start()

    @pl.loop(0, count)
    def _(n):
        load_x(n).start()
        load_c(n).start()

    def train(lo, hi):
        @pl.loop(lo, hi)
        def _(n):
            load_x(n).wait()
            load_c(n).wait()
            grad[n] = lax.dot_general(tc[n], tx[n], TN, preferred_element_type=F32).astype(BF16)

    def direct_c(i, p):
        k = base_c(0, 0) + 4 * i

        @pl.when(far(slot(k)))
        def _():
            qc_to_dp(k, i, p).wait_recv()
            qc_to_dp(k, i, p).start()
            qc_to_fisher(k, i, p, 2).start()

    def direct_x(i, p):
        j = base_x(0) + 2 * i

        @pl.when(j > 0)
        def _():
            qx_to_dp(j, i, p).wait_recv()
            qx_to_dp(j, i, p).start()
            qx_to_partner(j, i, p, 1).start()

    def second_c(i, p):
        k = base_c(1, 0) + 4 * i

        @pl.when(far(slot(k)))
        def _():
            qc_to_fisher(k, i, p, 3).wait_recv()
            qc_to_fisher(k, i, p, 3).start()

    def second_x(i, p):
        j = base_x(1) + 2 * i

        @pl.when(j > 0)
        def _():
            qx_to_partner(j, i, p, 3).wait_recv()
            qx_to_partner(j, i, p, 3).start()

    def choose():
        load_f.wait()
        for h in range(heads):
            rows = pl.ds(h * HEAD_WIDTH, HEAD_WIDTH)
            which = layer_ref[t * heads + h]
            chosen = jnp.zeros((HEAD_WIDTH, half), F32)
            for layer in range(stored):
                chosen += fw[layer, rows, :].astype(F32) * (which == layer).astype(F32)
            fw[0, rows, :] = chosen.astype(BF16)

    shift = pl.multiple_of(t * width - start_of(t), 16)

    def weigh(m):
        block[...] = lax.dot_general(qc[m], qx[m], TN, preferred_element_type=F32)
        weighted[m] = (fw[0].astype(F32) * block[pl.ds(shift, width), :]).astype(BF16)

    def last_c(flip, i):
        k = base_c(flip, 1) + 4 * i

        @pl.when(far(slot(k)))
        def _():
            for p in range(CHUNKS):
                qc_to_fisher(k, i, p, 2).wait_recv()

    def last_x(j):
        m = x_slot(j, 1)
        for p in range(CHUNKS):
            hop(qx, m, p, qx_send.at[0, 0, p], qx_recv, {"tensor": t_other}).wait_recv()

    steps = CHUNKS * c_steps + 2
    done = 0

    def some_train():
        nonlocal done
        train(count * done // steps, count * (done + 1) // steps)
        done += 1

    some_train()
    for p in range(CHUNKS):
        for i in range(c_steps):
            direct_c(i, p)
        for i in range(c_steps):
            if p > 0:
                second_c(i, p - 1)
            some_train()
    choose()
    for i in range(c_steps):
        second_c(i, CHUNKS - 1)
    own_c.wait()
    own_x.wait()
    for ref, sem in ((qc, qc_recv), (qx, qx_recv)):
        remote(
            ref.at[t_other],
            ref.at[t_other],
            own_send.at[0],
            sem.at[t_other, 0],
            {"tensor": t_other},
        ).wait_recv()
    some_train()
    for p in range(CHUNKS):
        direct_x(0, p)
        if p > 0:
            second_x(0, p - 1)
    second_x(0, CHUNKS - 1)
    weigh(t)
    weigh(t_other)
    for i in range(c_steps):
        for flip in range(2):
            last_c(flip, i)
    for i in range(x_steps):
        for p in range(CHUNKS if i + 1 < x_steps else 0):
            direct_x(i + 1, p)
            if p > 0:
                second_x(i + 1, p - 1)
        if i + 1 < x_steps:
            second_x(i + 1, CHUNKS - 1)
        for j in (2 * i, 2 * i + 1):
            if j > 0:
                last_x(j)
                weigh(x_slot(j, 0))
                weigh(x_slot(j, 1))

    rows_n, rows_m = count * RB, tensor_n * RB
    row_id = lax.broadcasted_iota(jnp.int32, (rows_n, rows_m), 0)
    col_id = lax.broadcasted_iota(jnp.int32, (rows_n, rows_m), 1)
    same = (lax.rem(row_id, RB) == lax.rem(col_id, RB)).astype(F32)
    train_hot = (
        lax.broadcasted_iota(jnp.int32, (groups * ids_dev, count), 0) == tid_ref[...]
    ).astype(F32)
    query_hot = (
        lax.broadcasted_iota(jnp.int32, (rows_m, LANES), 1) == qid_ref[...]
    ).astype(F32)
    part[...] = jnp.zeros_like(part)
    for h in range(heads):
        acc[...] = jnp.zeros_like(acc)

        @pl.loop(0, HEAD_WIDTH // RB)
        def _(i):
            rows = pl.ds(pl.multiple_of(h * HEAD_WIDTH + i * RB, RB), RB)
            left = grad[:, rows, :].reshape(rows_n, half)
            right = weighted[:, rows, :].reshape(rows_m, half)
            acc[...] += lax.dot_general(left, right, NT, preferred_element_type=F32)

        kept = (acc[...] * same).reshape(count, RB, rows_m).sum(axis=1)
        by_query = jnp.dot(
            kept, query_hot, preferred_element_type=F32, precision=lax.Precision.HIGHEST
        )
        buckets = (
            jnp.dot(
                train_hot, by_query, preferred_element_type=F32, precision=lax.Precision.HIGHEST
            )
            * scale
        )
        for g in range(groups):
            part[g, h, 0:ids_dev, :] = buckets[g * ids_dev : (g + 1) * ids_dev, :]

    def exchange(d):
        g = lax.rem(me + d, groups)
        to = {"dp": g // fisher_n, "fisher": lax.rem(g, fisher_n)}
        return remote(part.at[g], got.at[d], part_send.at[d], part_recv.at[d], to)

    for d in range(1, groups):
        exchange(d).start()
    total = part[me]
    for d in range(1, groups):
        exchange(d).wait_recv()
        total += got[d]
    out_ref[...] = total

    for d in range(1, groups):
        exchange(d).wait_send()
    qc_partner().wait_send()
    qx_partner().wait_send()
    for p in range(CHUNKS):
        for i in range(c_steps):
            k = base_c(0, 0) + 4 * i

            @pl.when(far(target(k)))
            def _(k=k, i=i, p=p):
                qc_first(k, i, p).wait_send()

            @pl.when(far(slot(k)))
            def _(k=k, i=i, p=p):
                qc_to_dp(k, i, p).wait_send()
                qc_to_fisher(k, i, p, 2).wait_send()

            k = base_c(1, 0) + 4 * i

            @pl.when(far(slot(k)))
            def _(k=k, i=i, p=p):
                qc_to_fisher(k, i, p, 3).wait_send()

        for i in range(x_steps):
            j = base_x(0) + 2 * i

            @pl.when(j > 0)
            def _(j=j, i=i, p=p):
                qx_first(j, i, p).wait_send()
                qx_to_dp(j, i, p).wait_send()
                qx_to_partner(j, i, p, 1).wait_send()

            j = base_x(1) + 2 * i

            @pl.when(j > 0)
            def _(j=j, i=i, p=p):
                qx_to_partner(j, i, p, 3).wait_send()


def local(axes, tx, tc, tids, qx, qc, qids, fw, layers):
    tensor_n, dp_n, fisher_n, ids_dev = axes
    count, seq, half = tx.shape
    width = tc.shape[2]
    heads = width // HEAD_WIDTH
    full = half * fisher_n
    scale = 1.0 / (seq * math.sqrt(HEAD_WIDTH * full))
    total_cols = qc.shape[2]
    win = 0
    for dest in range(tensor_n):
        lo = dest * width // LANES * LANES
        win = max(win, -(-(dest * width + width - lo) // LANES) * LANES)
    groups = dp_n * fisher_n
    sizes = (tensor_n, dp_n, fisher_n, win, ids_dev, scale)
    vmem = pl.BlockSpec(memory_space=pltpu.VMEM)
    hbm = pl.BlockSpec(memory_space=pl.ANY)
    dma = pltpu.SemaphoreType.DMA
    out = pl.pallas_call(
        functools.partial(kernel, sizes),
        out_shape=jax.ShapeDtypeStruct((heads, 8, LANES), F32),
        in_specs=[pl.BlockSpec(memory_space=pltpu.SMEM), hbm, hbm, hbm, hbm, hbm, vmem, vmem],
        out_specs=vmem,
        scratch_shapes=[
            pltpu.VMEM((count, seq, half), BF16),
            pltpu.VMEM((count, seq, width), BF16),
            pltpu.VMEM((count, width, half), BF16),
            pltpu.VMEM((tensor_n, seq, win), BF16),
            pltpu.VMEM((tensor_n, seq, half), BF16),
            pltpu.VMEM((tensor_n, width, half), BF16),
            pltpu.VMEM(fw.shape, BF16),
            pltpu.VMEM((win, half), F32),
            pltpu.VMEM((count * RB, tensor_n * RB), F32),
            pltpu.VMEM((groups, heads, 8, LANES), F32),
            pltpu.VMEM((groups, heads, 8, LANES), F32),
            dma((count,)),
            dma((count,)),
            dma,
            dma((2,)),
            dma((2,)),
            dma((tensor_n, CHUNKS)),
            dma((4, tensor_n // 4, CHUNKS)),
            dma((tensor_n, CHUNKS)),
            dma((4, tensor_n // 4, CHUNKS)),
            dma((groups,)),
            dma((groups,)),
        ],
        compiler_params=pltpu.CompilerParams(
            collective_id=0, has_side_effects=True, vmem_limit_bytes=60 * 1024 * 1024
        ),
    )(layers, tx, tc, qx, qc, fw, tids[None, :], jnp.repeat(qids, RB)[:, None])
    return jnp.transpose(out[:, :ids_dev, :QIDS], (1, 2, 0))


def solution(mesh):
    in_specs = (
        P("dp", None, "fisher"),
        P("dp", None, "tensor"),
        P("dp"),
        P("tensor", None, "fisher"),
        P("tensor", None, None),
        P(),
        P(None, "tensor", "fisher"),
        P(),
    )
    out_specs = P(("dp", "fisher"), None, "tensor")
    axes = (mesh.shape["tensor"], mesh.shape["dp"], mesh.shape["fisher"], 4)
    return jax.shard_map(
        functools.partial(local, axes),
        mesh=mesh,
        in_specs=in_specs,
        out_specs=out_specs,
        check_vma=False,
    )
```
